128 devices in a mesh: frame: 64 (over z, y, x), pix: 2 (over core).
Axes of the slice: x: 4, y: 4, z: 4, core: 2. Of those that a mesh axis runs over, the one named last changes fastest.
Arguments:
- frames: bfloat16 [1024, 131072], P('frame', 'pix'), as said below
- cycle_map: int32 [131072], P('pix'), may hold values from -1 to 63, as said below
Outputs:
- correlation: bfloat16 [64, 1024, 1024], P('frame', 'pix')
The draws below stay inside these ranges and needn't reach their ends.
Inputs may be any that keep to these rules, and one draw needn't show every extreme that they name: `frames`: every entry is positive. `cycle_map`: pixels come in aligned blocks of 128; every pixel of a block is either -1 or one common cycle, and the first pixel of a block that holds a cycle belongs to it. Within each sector (aligned blocks of 65536 pixels, one a pix group) every cycle holds at least one and at most 8 blocks, and every cycle holds exactly 1024 pixels in some sector.
All inputs are finite; a program needn't handle non-finite values.
Results may differ from the reference program's by a relative error of at most 0.012.
Values may be sent and summed in bfloat16 or wider, within the bound.
A program may use at most 64 MiB of HBM per device.

```python
import math
import jax
import jax.numpy as jnp
from jax import lax

F = 1024
BLOCK = 128
CAP = 1024
HALF_WIN = 2
CYCLES = 64
P_SEC = 65536
NPIX = 131072
N_PIX = 2


def draw_frames(key, part):
    key_scale, key_speckle, key_omega, key_phase, key_drift = jax.random.split(key, 5)
    frame_pos = jnp.arange(F, dtype=jnp.float32)[:, None]
    scale = jnp.exp(jax.random.uniform(key_scale, (1, NPIX), jnp.float32) * math.log(10.0))
    uniform_part = jax.random.uniform(key_speckle, (F, NPIX), jnp.float32)
    speckle = 0.05 - jnp.log(1.0 - 0.99 * uniform_part)
    omega = jnp.exp(jax.random.uniform(key_omega, (1, NPIX), jnp.float32, math.log(0.005), math.log(0.3)))
    phase = jax.random.uniform(key_phase, (1, NPIX), jnp.float32, -math.pi, math.pi)
    drift = jax.random.uniform(key_drift, (F, 1), jnp.float32, 0.7, 1.3)
    values = scale * drift * speckle * (1.0 + 0.5 * jnp.sin(omega * frame_pos + phase))
    return values.astype(jnp.bfloat16)


def draw_cycle_map(key, part):
    key_flip, key_jitter, key_keep, key_perm = jax.random.split(key, 4)
    block_count = P_SEC // BLOCK
    cap_blocks = CAP // BLOCK
    sector = jnp.arange(N_PIX, dtype=jnp.int32)[:, None]
    flip = jax.random.randint(key_flip, (1, CYCLES), 0, 2, dtype=jnp.int32)
    position = jnp.where(flip == 1, N_PIX - 1 - sector, sector)
    last = position == N_PIX - 1
    base = cap_blocks // 3 + (cap_blocks - cap_blocks // 3) * position // (N_PIX - 1)
    jitter = jax.random.randint(key_jitter, (N_PIX, CYCLES), 0, cap_blocks // 8 + 1, dtype=jnp.int32)
    blocks_used = jnp.where(last, cap_blocks, jnp.maximum(base - jitter, 1))
    threshold = jnp.where(last, 8, 3 + 5 * position // (N_PIX - 1))
    block_slot = jnp.arange(block_count, dtype=jnp.int32)
    cycle_of = block_slot // cap_blocks
    rank_of = block_slot % cap_blocks
    live_block = rank_of[None, :] < blocks_used[:, cycle_of]
    draws = jax.random.randint(key_keep, (N_PIX, block_count, BLOCK), 0, 8, dtype=jnp.int32)
    first_pixel = (jnp.arange(BLOCK, dtype=jnp.int32) == 0)[None, None, :]
    keep = (draws < threshold[:, cycle_of][:, :, None]) | first_pixel
    labels = jnp.where(live_block[:, :, None] & keep, cycle_of[None, :, None], -1)
    sector_keys = jax.random.split(key_perm, N_PIX)

    def shuffle(sector_key, sector_labels):
        return sector_labels[jax.random.permutation(sector_key, block_count)]
    mixed = jax.vmap(shuffle)(sector_keys, labels)
    return mixed.reshape(-1).astype(jnp.int32)


def setup_inputs(seed: int = 0) -> dict:
    arg_keys = jax.random.split(jax.random.key(seed), 3)
    frames = draw_frames(jax.random.fold_in(arg_keys[2], 71), 0)
    cycle_map = draw_cycle_map(jax.random.fold_in(arg_keys[2], 71), 0)
    return {"frames": frames, "cycle_map": cycle_map}


def window_sum(padded, length):
    summed = padded[0:length]
    for offset in range(1, 2 * HALF_WIN + 1):
        summed = summed + padded[offset:offset + length]
    return summed


def smooth_count(first_frame, length, total):
    frame_pos = first_frame + jnp.arange(length, dtype=jnp.int32)
    upper = jnp.minimum(frame_pos + HALF_WIN, total - 1)
    lower = jnp.maximum(frame_pos - HALF_WIN, 0)
    return (upper - lower + 1).astype(jnp.float32)


def reference(frames, cycle_map):
    ranking = jnp.argsort(cycle_map, stable=True).astype(jnp.int32)
    sorted_ids = cycle_map[ranking]
    cycle_ids = jnp.arange(CYCLES, dtype=jnp.int32)
    starts = jnp.searchsorted(sorted_ids, cycle_ids, side="left").astype(jnp.int32)
    finish = jnp.searchsorted(sorted_ids, cycle_ids, side="right").astype(jnp.int32)
    slot_count = N_PIX * CAP
    divisor = smooth_count(0, F, F)

    def one_cycle(cycle_index):
        first_slot = starts[cycle_index]
        members = finish[cycle_index] - first_slot
        within = jnp.arange(slot_count, dtype=jnp.int32)
        occupied = (within < members)[None, :]
        pixel_idx = ranking[jnp.minimum(first_slot + within, NPIX - 1)]
        raw_block = frames[:, pixel_idx].astype(jnp.float32)
        padded = jnp.pad(raw_block, ((HALF_WIN, HALF_WIN), (0, 0)))
        summed = window_sum(padded, F)
        local_mean = jnp.where(occupied, summed, jnp.float32(1.0)) / divisor[:, None]
        normed = jnp.where(occupied, raw_block / local_mean, jnp.float32(0.0)).astype(jnp.bfloat16)
        values = normed.astype(jnp.float32)
        gram_sum = jnp.dot(values, values.T, precision=lax.Precision.HIGHEST, preferred_element_type=jnp.float32)
        frame_sum = jnp.sum(values, axis=1)
        number = members.astype(jnp.float32)
        result = number * gram_sum / (frame_sum[:, None] * frame_sum[None, :]) - 1.0
        return result.astype(jnp.bfloat16)

    return lax.map(one_cycle, jnp.arange(CYCLES, dtype=jnp.int32))
```

```python
import functools

import jax
import jax.numpy as jnp
from jax import lax
from jax.experimental import pallas as pl
from jax.experimental.pallas import tpu as pltpu
from jax.sharding import PartitionSpec as P

BLOCK = 128
HALF_WIN = 2
PAD = 16
CHUNKS = 4
STRIDE = 27
MESH = pl.DeviceIdType.MESH


def kernel(
    cycles,
    frames_hbm,
    map_hbm,
    out_ref,
    fr,
    cmap,
    table_v,
    table,
    send,
    recv,
    own,
    oth,
    acc,
    rowacc,
    inv_len,
    band,
    mask,
    cnt_own,
    cnt_oth,
    load_sem,
    send_sem,
    recv_sem,
    swap_send,
    swap_recv,
    cnt_sem,
):
    f = lax.axis_index("frame")
    p = lax.axis_index("pix")
    fr_dev = frames_hbm.shape[0]
    p_sec = frames_hbm.shape[1]
    blocks = p_sec // BLOCK
    total = fr_dev * cycles
    rows = total // 2
    slots = p_sec // cycles // BLOCK
    per = slots // CHUNKS
    width = per * BLOCK
    tile = min(256, total)

    map_copy = pltpu.make_async_copy(map_hbm, cmap.at[pl.ds(0, blocks)], load_sem.at[0])
    map_copy.start()
    fr_copy = pltpu.make_async_copy(frames_hbm, fr.at[:, pl.ds(0, p_sec)], load_sem.at[1])
    fr_copy.start()

    barrier = pltpu.get_barrier_semaphore()

    def greet(i, carry):
        peer = lax.rem(f + STRIDE * i, cycles)
        pl.semaphore_signal(barrier, inc=1, device_id=(peer, p), device_id_type=MESH)
        return carry

    lax.fori_loop(1, cycles, greet, 0)
    pl.semaphore_signal(barrier, inc=1, device_id=(f, 1 - p), device_id_type=MESH)

    fr[:, pl.ds(p_sec, BLOCK)] = jnp.zeros((fr_dev, BLOCK), jnp.bfloat16)
    cmap[pl.ds(blocks, 8), :] = jnp.full((8, BLOCK), -1, jnp.int32)
    map_copy.wait()
    lane = lax.broadcasted_iota(jnp.int32, (8, BLOCK), 1)
    lead = lax.broadcasted_iota(jnp.int32, (8, BLOCK), 0)
    running = jnp.zeros((8, BLOCK), jnp.int32)
    member = []
    before = []
    for v in range(blocks // 8):
        member.append(jnp.broadcast_to(cmap[pl.ds(8 * v, 8), 0:1], (8, BLOCK)) == lane)
        before.append(running)
        running = running + jnp.where(member[v], 1, 0)
    ahead = [jnp.zeros((1, BLOCK), jnp.int32)]
    for i in range(7):
        ahead.append(ahead[i] + running[i : i + 1, :])
    ahead = jnp.concatenate(ahead, axis=0)
    picks = [jnp.zeros((8, BLOCK), jnp.int32)] * slots
    for v in range(blocks // 8):
        rank = jnp.where(member[v], before[v] + ahead, -1)
        for r in range(slots):
            picks[r] = picks[r] + jnp.where(rank == r, lead + (8 * v + 1), 0)
    found = jnp.concatenate([jnp.sum(x, axis=0, keepdims=True) for x in picks], axis=0)
    table_v[...] = jnp.where(found > 0, found - 1, blocks)
    table_copy = pltpu.make_async_copy(table_v, table, load_sem.at[2])
    table_copy.start()
    table_copy.wait()
    fr_copy.wait()

    def pick(k):
        def one(q, carry):
            for j in range(per):
                b = table[k * per + j, q]
                send[k, pl.ds(pl.multiple_of(q * fr_dev, fr_dev), fr_dev), pl.ds(j * BLOCK, BLOCK)] = fr[
                    :, pl.ds(b * BLOCK, BLOCK)
                ]
            return carry

        lax.fori_loop(0, cycles, one, 0, unroll=8 if cycles % 8 == 0 else 1)

    def ship(k):
        def one(i, carry):
            peer = lax.rem(f + STRIDE * i, cycles)
            pltpu.make_async_remote_copy(
                src_ref=send.at[k, pl.ds(pl.multiple_of(peer * fr_dev, fr_dev), fr_dev)],
                dst_ref=recv.at[k, pl.ds(pl.multiple_of(PAD + f * fr_dev, fr_dev), fr_dev)],
                send_sem=send_sem.at[k],
                recv_sem=recv_sem.at[k],
                device_id=(peer, p),
                device_id_type=MESH,
            ).start()
            return carry

        lax.fori_loop(1, cycles, one, 0)
        recv[k, pl.ds(pl.multiple_of(PAD + f * fr_dev, fr_dev), fr_dev), :] = send[
            k, pl.ds(pl.multiple_of(f * fr_dev, fr_dev), fr_dev), :
        ]

    pick(0)
    pl.semaphore_wait(barrier, cycles)
    ship(0)
    for k in range(1, CHUNKS):
        pick(k)
        ship(k)

    number = jnp.zeros((1, BLOCK), jnp.float32)
    for r in range(slots):
        row = (cmap[pl.ds(table[r, f], 1), :] == f).astype(jnp.float32)
        number = number + row
        mask[:, pl.ds(r * BLOCK, BLOCK)] = jnp.broadcast_to(row, (8, BLOCK))
    cnt_own[...] = jnp.broadcast_to(jnp.sum(number, axis=1, keepdims=True), (8, BLOCK))
    cnt_copy = pltpu.make_async_remote_copy(
        src_ref=cnt_own,
        dst_ref=cnt_oth,
        send_sem=cnt_sem.at[0],
        recv_sem=cnt_sem.at[1],
        device_id=(f, 1 - p),
        device_id_type=MESH,
    )
    cnt_copy.start()

    zero_pad = jnp.zeros((PAD, width), jnp.bfloat16)
    for k in range(CHUNKS):
        recv[k, pl.ds(0, PAD), :] = zero_pad
        recv[k, pl.ds(PAD + total, PAD), :] = zero_pad
    pos = lax.broadcasted_iota(jnp.int32, (total, BLOCK), 0)
    frames_in = jnp.minimum(pos + HALF_WIN, total - 1) - jnp.maximum(pos - HALF_WIN, 0) + 1
    inv_len[...] = 1.0 / frames_in.astype(jnp.float32)
    away = lax.broadcasted_iota(jnp.int32, (tile, tile + 2 * PAD), 1) - PAD - lax.broadcasted_iota(
        jnp.int32, (tile, tile + 2 * PAD), 0
    )
    band[...] = (jnp.abs(away) <= HALF_WIN).astype(jnp.float32).astype(jnp.bfloat16)
    ones_rows = jnp.ones((PAD, width), jnp.bfloat16)
    ones_cols = jnp.ones((width, BLOCK), jnp.bfloat16)
    first_row = pl.multiple_of(p * rows, rows)

    def normalise(k):
        valid = mask[0:1, pl.ds(k * width, width)] > 0.0

        for j in range(total // tile):
            start = j * tile
            summed = jnp.dot(
                band[...], recv[k, pl.ds(start, tile + 2 * PAD), :], preferred_element_type=jnp.float32
            )
            scale = inv_len[pl.ds(start, tile), :]
            mean = summed * jnp.concatenate([scale] * per, axis=1)
            value = recv[k, pl.ds(start + PAD, tile), :].astype(jnp.float32)
            normed = jnp.where(valid, value / mean, 0.0)
            own[k, pl.ds(start, tile), :] = normed.astype(jnp.bfloat16)
            pltpu.make_async_remote_copy(
                src_ref=own.at[k, pl.ds(start, tile)],
                dst_ref=oth.at[k, pl.ds(start, tile)],
                send_sem=swap_send.at[k],
                recv_sem=swap_recv.at[k],
                device_id=(f, 1 - p),
                device_id_type=MESH,
            ).start()

    def products(ref, k, n):
        left = jnp.concatenate([ref[k, pl.ds(first_row, rows), :], ones_rows], axis=0)
        return lax.dot_general(
            left,
            ref[k, pl.ds(n * tile, tile), :],
            (((1,), (1,)), ((), ())),
            preferred_element_type=jnp.float32,
        )

    def row_sums(ref, k):
        return jnp.dot(
            ref[k, pl.ds(first_row, rows), :], ones_cols, preferred_element_type=jnp.float32
        )

    def gram(ref, k, first):
        rowacc[...] = row_sums(ref, k) if first else rowacc[...] + row_sums(ref, k)
        for n in range(total // tile):
            columns = pl.ds(n * tile, tile)
            term = products(ref, k, n)
            acc[:, columns] = term if first else acc[:, columns] + term

    def swapped(k):
        pltpu.make_async_copy(own.at[k], oth.at[k], swap_recv.at[k]).wait()

    for k in range(CHUNKS):
        arrived = recv.at[k, pl.ds(0, total - fr_dev)]
        pltpu.make_async_copy(arrived, arrived, recv_sem.at[k]).wait()
        normalise(k)
        if k > 0:
            swapped(k - 1)
            gram(oth, k - 1, False)
        gram(own, k, k == 0)

    last = CHUNKS - 1
    cnt_copy.wait()
    members = cnt_own[0:1, 0:1] + cnt_oth[0:1, 0:1]
    swapped(last)
    row_total = rowacc[...] + row_sums(oth, last)
    row_total = jnp.concatenate([row_total] * (tile // BLOCK), axis=1) if tile > BLOCK else row_total[:, :tile]
    for n in range(total // tile):
        sums = acc[:, pl.ds(n * tile, tile)] + products(oth, last, n)
        col_total = sums[rows : rows + 1, :]
        result = members * sums[:rows] / (row_total * col_total) - 1.0
        out_ref[:, pl.ds(n * tile, tile)] = result.astype(jnp.bfloat16)

    for k in range(CHUNKS):
        sent = send.at[k, pl.ds(0, total - fr_dev)]
        pltpu.make_async_copy(sent, sent, send_sem.at[k]).wait()
        pltpu.make_async_copy(own.at[k], oth.at[k], swap_send.at[k]).wait()


def body(frames, cycle_map):
    fr_dev, p_sec = frames.shape
    cycles = lax.axis_size("frame")
    total = fr_dev * cycles
    blocks = p_sec // BLOCK
    rows = total // lax.axis_size("pix")
    cap = p_sec // cycles
    slots = cap // BLOCK
    width = cap // CHUNKS
    tile = min(256, total)
    dma = pltpu.SemaphoreType.DMA
    out = pl.pallas_call(
        functools.partial(kernel, cycles),
        out_shape=jax.ShapeDtypeStruct((rows, total), jnp.bfloat16),
        in_specs=[pl.BlockSpec(memory_space=pltpu.HBM)] * 2,
        out_specs=pl.BlockSpec(memory_space=pltpu.VMEM),
        scratch_shapes=[
            pltpu.VMEM((fr_dev, p_sec + BLOCK), jnp.bfloat16),
            pltpu.VMEM((blocks + 8, BLOCK), jnp.int32),
            pltpu.VMEM((slots, BLOCK), jnp.int32),
            pltpu.SMEM((slots, BLOCK), jnp.int32),
            pltpu.VMEM((CHUNKS, total, width), jnp.bfloat16),
            pltpu.VMEM((CHUNKS, total + 2 * PAD, width), jnp.bfloat16),
            pltpu.VMEM((CHUNKS, total, width), jnp.bfloat16),
            pltpu.VMEM((CHUNKS, total, width), jnp.bfloat16),
            pltpu.VMEM((rows + PAD, total), jnp.float32),
            pltpu.VMEM((rows, BLOCK), jnp.float32),
            pltpu.VMEM((total, BLOCK), jnp.float32),
            pltpu.VMEM((tile, tile + 2 * PAD), jnp.bfloat16),
            pltpu.VMEM((8, cap), jnp.float32),
            pltpu.VMEM((8, BLOCK), jnp.float32),
            pltpu.VMEM((8, BLOCK), jnp.float32),
            dma((3,)),
            dma((CHUNKS,)),
            dma((CHUNKS,)),
            dma((CHUNKS,)),
            dma((CHUNKS,)),
            dma((2,)),
        ],
        compiler_params=pltpu.CompilerParams(
            collective_id=0, has_side_effects=True, vmem_limit_bytes=60 << 20
        ),
    )(frames, cycle_map.reshape(blocks, BLOCK))
    return out[None]


def solution(mesh):
    return jax.shard_map(
        body,
        mesh=mesh,
        in_specs=(P("frame", "pix"), P("pix")),
        out_specs=P("frame", "pix", None),
        check_vma=False,
    )
```

```python
import functools

import jax
import jax.numpy as jnp
from jax import lax
from jax.experimental import pallas as pl
from jax.experimental.pallas import tpu as pltpu
from jax.sharding import PartitionSpec as P

BLOCK = 128
HALF_WIN = 2
PAD = 16
SPLIT = (3, 3, 2)
STRIDE = 27
MESH = pl.DeviceIdType.MESH


def chunks_of(slots):
    sizes = [size * slots // sum(SPLIT) for size in SPLIT]
    return [(sum(sizes[:k]), size) for k, size in enumerate(sizes)]


def kernel(
    cycles,
    frames_hbm,
    map_hbm,
    out_ref,
    fr,
    cmap,
    table_v,
    table,
    *refs,
):
    f = lax.axis_index("frame")
    p = lax.axis_index("pix")
    fr_dev = frames_hbm.shape[0]
    p_sec = frames_hbm.shape[1]
    blocks = p_sec // BLOCK
    total = fr_dev * cycles
    rows = total // 2
    slots = p_sec // cycles // BLOCK
    chunks = chunks_of(slots)
    count = len(chunks)
    tile = min(256, total)
    send, recv, own, oth = (refs[i * count : (i + 1) * count] for i in range(4))
    (
        acc,
        rowacc,
        inv_len,
        band,
        mask,
        cnt_own,
        cnt_oth,
        load_sem,
        send_sem,
        recv_sem,
        swap_send,
        swap_recv,
        cnt_sem,
    ) = refs[4 * count :]

    map_copy = pltpu.make_async_copy(map_hbm, cmap.at[pl.ds(0, blocks)], load_sem.at[0])
    map_copy.start()
    fr_copy = pltpu.make_async_copy(frames_hbm, fr.at[:, pl.ds(0, p_sec)], load_sem.at[1])
    fr_copy.start()

    barrier = pltpu.get_barrier_semaphore()

    def greet(i, carry):
        peer = lax.rem(f + STRIDE * i, cycles)
        pl.semaphore_signal(barrier, inc=1, device_id=(peer, p), device_id_type=MESH)
        return carry

    lax.fori_loop(1, cycles, greet, 0)
    pl.semaphore_signal(barrier, inc=1, device_id=(f, 1 - p), device_id_type=MESH)

    fr[:, pl.ds(p_sec, BLOCK)] = jnp.zeros((fr_dev, BLOCK), jnp.bfloat16)
    cmap[pl.ds(blocks, 8), :] = jnp.full((8, BLOCK), -1, jnp.int32)
    map_copy.wait()
    lane = lax.broadcasted_iota(jnp.int32, (8, BLOCK), 1)
    lead = lax.broadcasted_iota(jnp.int32, (8, BLOCK), 0)
    running = jnp.zeros((8, BLOCK), jnp.int32)
    member = []
    before = []
    for v in range(blocks // 8):
        member.append(jnp.broadcast_to(cmap[pl.ds(8 * v, 8), 0:1], (8, BLOCK)) == lane)
        before.append(running)
        running = running + jnp.where(member[v], 1, 0)
    ahead = [jnp.zeros((1, BLOCK), jnp.int32)]
    for i in range(7):
        ahead.append(ahead[i] + running[i : i + 1, :])
    ahead = jnp.concatenate(ahead, axis=0)
    picks = [jnp.zeros((8, BLOCK), jnp.int32)] * slots
    for v in range(blocks // 8):
        rank = jnp.where(member[v], before[v] + ahead, -1)
        for r in range(slots):
            picks[r] = picks[r] + jnp.where(rank == r, lead + (8 * v + 1), 0)
    found = jnp.concatenate([jnp.sum(x, axis=0, keepdims=True) for x in picks], axis=0)
    table_v[...] = jnp.where(found > 0, found - 1, blocks)
    table_copy = pltpu.make_async_copy(table_v, table, load_sem.at[2])
    table_copy.start()
    table_copy.wait()
    fr_copy.wait()

    def pick(k):
        def one(q, carry):
            for j in range(chunks[k][1]):
                b = table[chunks[k][0] + j, q]
                send[k][pl.ds(pl.multiple_of(q * fr_dev, fr_dev), fr_dev), pl.ds(j * BLOCK, BLOCK)] = fr[
                    :, pl.ds(b * BLOCK, BLOCK)
                ]
            return carry

        lax.fori_loop(0, cycles, one, 0, unroll=8 if cycles % 8 == 0 else 1)

    def ship(k):
        def one(i, carry):
            peer = lax.rem(f + STRIDE * i, cycles)
            pltpu.make_async_remote_copy(
                src_ref=send[k].at[pl.ds(pl.multiple_of(peer * fr_dev, fr_dev), fr_dev)],
                dst_ref=recv[k].at[pl.ds(pl.multiple_of(PAD + f * fr_dev, fr_dev), fr_dev)],
                send_sem=send_sem.at[k],
                recv_sem=recv_sem.at[k],
                device_id=(peer, p),
                device_id_type=MESH,
            ).start()
            return carry

        lax.fori_loop(1, cycles, one, 0)
        recv[k][pl.ds(pl.multiple_of(PAD + f * fr_dev, fr_dev), fr_dev), :] = send[k][
            pl.ds(pl.multiple_of(f * fr_dev, fr_dev), fr_dev), :
        ]

    pick(0)
    pl.semaphore_wait(barrier, cycles)
    ship(0)
    for k in range(1, count):
        pick(k)
        ship(k)

    number = jnp.zeros((1, BLOCK), jnp.float32)
    for r in range(slots):
        row = (cmap[pl.ds(table[r, f], 1), :] == f).astype(jnp.float32)
        number = number + row
        mask[:, pl.ds(r * BLOCK, BLOCK)] = jnp.broadcast_to(row, (8, BLOCK))
    cnt_own[...] = jnp.broadcast_to(jnp.sum(number, axis=1, keepdims=True), (8, BLOCK))
    cnt_copy = pltpu.make_async_remote_copy(
        src_ref=cnt_own,
        dst_ref=cnt_oth,
        send_sem=cnt_sem.at[0],
        recv_sem=cnt_sem.at[1],
        device_id=(f, 1 - p),
        device_id_type=MESH,
    )
    cnt_copy.start()

    for k in range(count):
        zero_pad = jnp.zeros((PAD, chunks[k][1] * BLOCK), jnp.bfloat16)
        recv[k][pl.ds(0, PAD), :] = zero_pad
        recv[k][pl.ds(PAD + total, PAD), :] = zero_pad
    pos = lax.broadcasted_iota(jnp.int32, (total, BLOCK), 0)
    frames_in = jnp.minimum(pos + HALF_WIN, total - 1) - jnp.maximum(pos - HALF_WIN, 0) + 1
    inv_len[...] = 1.0 / frames_in.astype(jnp.float32)
    away = lax.broadcasted_iota(jnp.int32, (tile, tile + 2 * PAD), 1) - PAD - lax.broadcasted_iota(
        jnp.int32, (tile, tile + 2 * PAD), 0
    )
    band[...] = (jnp.abs(away) <= HALF_WIN).astype(jnp.float32).astype(jnp.bfloat16)
    first_row = pl.multiple_of(p * rows, rows)

    def normalise(k):
        valid = mask[0:1, pl.ds(chunks[k][0] * BLOCK, chunks[k][1] * BLOCK)] > 0.0

        for j in range(total // tile):
            start = j * tile
            summed = jnp.dot(
                band[...], recv[k][pl.ds(start, tile + 2 * PAD), :], preferred_element_type=jnp.float32
            )
            scale = inv_len[pl.ds(start, tile), :]
            mean = summed * jnp.concatenate([scale] * chunks[k][1], axis=1)
            value = recv[k][pl.ds(start + PAD, tile), :].astype(jnp.float32)
            normed = jnp.where(valid, value / mean, 0.0)
            own[k][pl.ds(start, tile), :] = normed.astype(jnp.bfloat16)
            pltpu.make_async_remote_copy(
                src_ref=own[k].at[pl.ds(start, tile)],
                dst_ref=oth[k].at[pl.ds(start, tile)],
                send_sem=swap_send.at[k],
                recv_sem=swap_recv.at[k],
                device_id=(f, 1 - p),
                device_id_type=MESH,
            ).start()

    def products(ref, k, n):
        ones_rows = jnp.ones((PAD, ref[k].shape[1]), jnp.bfloat16)
        left = jnp.concatenate([ref[k][pl.ds(first_row, rows), :], ones_rows], axis=0)
        return lax.dot_general(
            left,
            ref[k][pl.ds(n * tile, tile), :],
            (((1,), (1,)), ((), ())),
            preferred_element_type=jnp.float32,
        )

    def row_sums(ref, k):
        ones_cols = jnp.ones((ref[k].shape[1], BLOCK), jnp.bfloat16)
        return jnp.dot(
            ref[k][pl.ds(first_row, rows), :], ones_cols, preferred_element_type=jnp.float32
        )

    def gram(ref, k, first):
        rowacc[...] = row_sums(ref, k) if first else rowacc[...] + row_sums(ref, k)
        for n in range(total // tile):
            columns = pl.ds(n * tile, tile)
            term = products(ref, k, n)
            acc[:, columns] = term if first else acc[:, columns] + term

    def swapped(k):
        pltpu.make_async_copy(own[k], oth[k], swap_recv.at[k]).wait()

    for k in range(count):
        arrived = recv[k].at[pl.ds(0, total - fr_dev)]
        pltpu.make_async_copy(arrived, arrived, recv_sem.at[k]).wait()
        normalise(k)
        if k > 0:
            swapped(k - 1)
            gram(oth, k - 1, False)
        gram(own, k, k == 0)

    last = count - 1
    cnt_copy.wait()
    members = cnt_own[0:1, 0:1] + cnt_oth[0:1, 0:1]
    swapped(last)
    row_total = rowacc[...] + row_sums(oth, last)
    row_total = jnp.concatenate([row_total] * (tile // BLOCK), axis=1) if tile > BLOCK else row_total[:, :tile]
    for n in range(total // tile):
        sums = acc[:, pl.ds(n * tile, tile)] + products(oth, last, n)
        col_total = sums[rows : rows + 1, :]
        result = members * sums[:rows] / (row_total * col_total) - 1.0
        out_ref[:, pl.ds(n * tile, tile)] = result.astype(jnp.bfloat16)

    for k in range(count):
        sent = send[k].at[pl.ds(0, total - fr_dev)]
        pltpu.make_async_copy(sent, sent, send_sem.at[k]).wait()
        pltpu.make_async_copy(own[k], oth[k], swap_send.at[k]).wait()


def body(frames, cycle_map):
    fr_dev, p_sec = frames.shape
    cycles = lax.axis_size("frame")
    total = fr_dev * cycles
    blocks = p_sec // BLOCK
    rows = total // lax.axis_size("pix")
    cap = p_sec // cycles
    slots = cap // BLOCK
    chunks = chunks_of(slots)
    widths = [size * BLOCK for first, size in chunks]
    tile = min(256, total)
    dma = pltpu.SemaphoreType.DMA
    out = pl.pallas_call(
        functools.partial(kernel, cycles),
        out_shape=pltpu.VMEM((rows, total), jnp.bfloat16),
        in_specs=[pl.BlockSpec(memory_space=pltpu.HBM)] * 2,
        out_specs=pl.BlockSpec(memory_space=pltpu.VMEM),
        scratch_shapes=[
            pltpu.VMEM((fr_dev, p_sec + BLOCK), jnp.bfloat16),
            pltpu.VMEM((blocks + 8, BLOCK), jnp.int32),
            pltpu.VMEM((slots, BLOCK), jnp.int32),
            pltpu.SMEM((slots, BLOCK), jnp.int32),
            *[pltpu.VMEM((total, width), jnp.bfloat16) for width in widths],
            *[pltpu.VMEM((total + 2 * PAD, width), jnp.bfloat16) for width in widths],
            *[pltpu.VMEM((total, width), jnp.bfloat16) for width in widths],
            *[pltpu.VMEM((total, width), jnp.bfloat16) for width in widths],
            pltpu.VMEM((rows + PAD, total), jnp.float32),
            pltpu.VMEM((rows, BLOCK), jnp.float32),
            pltpu.VMEM((total, BLOCK), jnp.float32),
            pltpu.VMEM((tile, tile + 2 * PAD), jnp.bfloat16),
            pltpu.VMEM((8, cap), jnp.float32),
            pltpu.VMEM((8, BLOCK), jnp.float32),
            pltpu.VMEM((8, BLOCK), jnp.float32),
            dma((3,)),
            dma((len(chunks),)),
            dma((len(chunks),)),
            dma((len(chunks),)),
            dma((len(chunks),)),
            dma((2,)),
        ],
        compiler_params=pltpu.CompilerParams(
            collective_id=0, has_side_effects=True, vmem_limit_bytes=60 << 20
        ),
    )(frames, cycle_map.reshape(blocks, BLOCK))
    return out[None]


def solution(mesh):
    return jax.shard_map(
        body,
        mesh=mesh,
        in_specs=(P("frame", "pix"), P("pix")),
        out_specs=P("frame", "pix", None),
        check_vma=False,
    )
```

```python
import functools

import jax
import jax.numpy as jnp
from jax import lax
from jax.experimental import pallas as pl
from jax.experimental.pallas import tpu as pltpu
from jax.sharding import PartitionSpec as P

BLOCK = 128
HALF_WIN = 2
PAD = 16
SPLIT = (2, 2, 2, 2)
STRIDE = 27
MESH = pl.DeviceIdType.MESH


def chunks_of(slots):
    sizes = [size * slots // sum(SPLIT) for size in SPLIT]
    return [(sum(sizes[:k]), size) for k, size in enumerate(sizes)]


def kernel(
    cycles,
    frames_hbm,
    map_hbm,
    out_ref,
    fr,
    cmap,
    table_v,
    table,
    *refs,
):
    f = lax.axis_index("frame")
    p = lax.axis_index("pix")
    fr_dev = frames_hbm.shape[0]
    p_sec = frames_hbm.shape[1]
    blocks = p_sec // BLOCK
    total = fr_dev * cycles
    rows = total // 2
    slots = p_sec // cycles // BLOCK
    chunks = chunks_of(slots)
    count = len(chunks)
    tile = min(256, total)
    send, recv, own, oth = (refs[i * count : (i + 1) * count] for i in range(4))
    (
        acc,
        rowacc,
        inv_len,
        band,
        mask,
        cnt_own,
        cnt_oth,
        load_sem,
        send_sem,
        recv_sem,
        swap_send,
        swap_recv,
        cnt_sem,
    ) = refs[4 * count :]

    map_copy = pltpu.make_async_copy(map_hbm, cmap.at[pl.ds(0, blocks)], load_sem.at[0])
    map_copy.start()
    fr_copy = pltpu.make_async_copy(frames_hbm, fr.at[:, pl.ds(0, p_sec)], load_sem.at[1])
    fr_copy.start()

    barrier = pltpu.get_barrier_semaphore()

    def greet(i, carry):
        peer = lax.rem(f + STRIDE * i, cycles)
        pl.semaphore_signal(barrier, inc=1, device_id=(peer, p), device_id_type=MESH)
        return carry

    steps = 7 if cycles % 7 == 1 else 1
    lax.fori_loop(1, cycles, greet, 0, unroll=steps)
    pl.semaphore_signal(barrier, inc=1, device_id=(f, 1 - p), device_id_type=MESH)

    fr[:, pl.ds(p_sec, BLOCK)] = jnp.zeros((fr_dev, BLOCK), jnp.bfloat16)
    cmap[pl.ds(blocks, 8), :] = jnp.full((8, BLOCK), -1, jnp.int32)
    map_copy.wait()
    lane = lax.broadcasted_iota(jnp.int32, (8, BLOCK), 1)
    lead = lax.broadcasted_iota(jnp.int32, (8, BLOCK), 0)
    running = jnp.zeros((8, BLOCK), jnp.int32)
    member = []
    before = []
    for v in range(blocks // 8):
        member.append(jnp.broadcast_to(cmap[pl.ds(8 * v, 8), 0:1], (8, BLOCK)) == lane)
        before.append(running)
        running = running + jnp.where(member[v], 1, 0)
    ahead = [jnp.zeros((1, BLOCK), jnp.int32)]
    for i in range(7):
        ahead.append(ahead[i] + running[i : i + 1, :])
    ahead = jnp.concatenate(ahead, axis=0)
    picks = [jnp.zeros((8, BLOCK), jnp.int32)] * slots
    for v in range(blocks // 8):
        rank = jnp.where(member[v], before[v] + ahead, -1)
        for r in range(slots):
            picks[r] = picks[r] + jnp.where(rank == r, lead + (8 * v + 1), 0)
    found = jnp.concatenate([jnp.sum(x, axis=0, keepdims=True) for x in picks], axis=0)
    table_v[...] = jnp.where(found > 0, found - 1, blocks)
    table_copy = pltpu.make_async_copy(table_v, table, load_sem.at[2])
    table_copy.start()
    table_copy.wait()
    fr_copy.wait()

    def pick(k):
        def one(q, carry):
            for j in range(chunks[k][1]):
                b = table[chunks[k][0] + j, q]
                send[k][pl.ds(pl.multiple_of(q * fr_dev, fr_dev), fr_dev), pl.ds(j * BLOCK, BLOCK)] = fr[
                    :, pl.ds(b * BLOCK, BLOCK)
                ]
            return carry

        lax.fori_loop(0, cycles, one, 0, unroll=8 if cycles % 8 == 0 else 1)

    def ship(k):
        def one(i, carry):
            peer = lax.rem(f + STRIDE * i, cycles)
            pltpu.make_async_remote_copy(
                src_ref=send[k].at[pl.ds(pl.multiple_of(peer * fr_dev, fr_dev), fr_dev)],
                dst_ref=recv[k].at[pl.ds(pl.multiple_of(PAD + f * fr_dev, fr_dev), fr_dev)],
                send_sem=send_sem.at[k],
                recv_sem=recv_sem.at[k],
                device_id=(peer, p),
                device_id_type=MESH,
            ).start()
            return carry

        lax.fori_loop(1, cycles, one, 0, unroll=steps)
        recv[k][pl.ds(pl.multiple_of(PAD + f * fr_dev, fr_dev), fr_dev), :] = send[k][
            pl.ds(pl.multiple_of(f * fr_dev, fr_dev), fr_dev), :
        ]

    pick(0)
    pl.semaphore_wait(barrier, cycles)
    ship(0)
    for k in range(1, count):
        pick(k)
        ship(k)

    number = jnp.zeros((1, BLOCK), jnp.float32)
    for r in range(slots):
        row = (cmap[pl.ds(table[r, f], 1), :] == f).astype(jnp.float32)
        number = number + row
        mask[:, pl.ds(r * BLOCK, BLOCK)] = jnp.broadcast_to(row, (8, BLOCK))
    cnt_own[...] = jnp.broadcast_to(jnp.sum(number, axis=1, keepdims=True), (8, BLOCK))
    cnt_copy = pltpu.make_async_remote_copy(
        src_ref=cnt_own,
        dst_ref=cnt_oth,
        send_sem=cnt_sem.at[0],
        recv_sem=cnt_sem.at[1],
        device_id=(f, 1 - p),
        device_id_type=MESH,
    )
    cnt_copy.start()

    for k in range(count):
        zero_pad = jnp.zeros((PAD, chunks[k][1] * BLOCK), jnp.bfloat16)
        recv[k][pl.ds(0, PAD), :] = zero_pad
        recv[k][pl.ds(PAD + total, PAD), :] = zero_pad
    pos = lax.broadcasted_iota(jnp.int32, (total, BLOCK), 0)
    frames_in = jnp.minimum(pos + HALF_WIN, total - 1) - jnp.maximum(pos - HALF_WIN, 0) + 1
    inv_len[...] = 1.0 / frames_in.astype(jnp.float32)
    away = lax.broadcasted_iota(jnp.int32, (tile, tile + 2 * PAD), 1) - PAD - lax.broadcasted_iota(
        jnp.int32, (tile, tile + 2 * PAD), 0
    )
    band[...] = (jnp.abs(away) <= HALF_WIN).astype(jnp.float32).astype(jnp.bfloat16)
    first_row = pl.multiple_of(p * rows, rows)

    def normalise(k):
        valid = mask[0:1, pl.ds(chunks[k][0] * BLOCK, chunks[k][1] * BLOCK)] > 0.0

        for j in range(total // tile):
            start = j * tile
            summed = jnp.dot(
                band[...], recv[k][pl.ds(start, tile + 2 * PAD), :], preferred_element_type=jnp.float32
            )
            scale = inv_len[pl.ds(start, tile), :]
            mean = summed * jnp.concatenate([scale] * chunks[k][1], axis=1)
            value = recv[k][pl.ds(start + PAD, tile), :].astype(jnp.float32)
            normed = jnp.where(valid, value / mean, 0.0)
            own[k][pl.ds(start, tile), :] = normed.astype(jnp.bfloat16)
            pltpu.make_async_remote_copy(
                src_ref=own[k].at[pl.ds(start, tile)],
                dst_ref=oth[k].at[pl.ds(start, tile)],
                send_sem=swap_send.at[k],
                recv_sem=swap_recv.at[k],
                device_id=(f, 1 - p),
                device_id_type=MESH,
            ).start()

    def side_by_side(parts, start, length):
        return jnp.concatenate([ref[pl.ds(start, length), :] for ref in parts], axis=1)

    def products(parts, n):
        left = side_by_side(parts, first_row, rows)
        ones_rows = jnp.ones((PAD, left.shape[1]), jnp.bfloat16)
        return lax.dot_general(
            jnp.concatenate([left, ones_rows], axis=0),
            side_by_side(parts, n * tile, tile),
            (((1,), (1,)), ((), ())),
            preferred_element_type=jnp.float32,
        )

    def row_sums(parts):
        left = side_by_side(parts, first_row, rows)
        ones_cols = jnp.ones((left.shape[1], BLOCK), jnp.bfloat16)
        return jnp.dot(left, ones_cols, preferred_element_type=jnp.float32)

    def gram(parts, first):
        rowacc[...] = row_sums(parts) if first else rowacc[...] + row_sums(parts)
        for n in range(total // tile):
            columns = pl.ds(n * tile, tile)
            term = products(parts, n)
            acc[:, columns] = term if first else acc[:, columns] + term

    def swapped(k):
        pltpu.make_async_copy(own[k], oth[k], swap_recv.at[k]).wait()

    for k in range(count):
        arrived = recv[k].at[pl.ds(0, total - fr_dev)]
        pltpu.make_async_copy(arrived, arrived, recv_sem.at[k]).wait()
        normalise(k)
        if k > 0:
            swapped(k - 1)
        gram([own[k]] if k == 0 else [oth[k - 1], own[k]], k == 0)

    last = count - 1
    cnt_copy.wait()
    members = cnt_own[0:1, 0:1] + cnt_oth[0:1, 0:1]
    swapped(last)
    row_total = rowacc[...] + row_sums([oth[last]])
    if tile > BLOCK:
        row_total = jnp.concatenate([row_total] * (tile // BLOCK), axis=1)
    else:
        row_total = row_total[:, :tile]
    for n in range(total // tile):
        columns = pl.ds(n * tile, tile)
        sums = acc[:, columns] + products([oth[last]], n)
        result = members * sums[:rows] / (row_total * sums[rows : rows + 1, :]) - 1.0
        out_ref[:, columns] = result.astype(jnp.bfloat16)

    for k in range(count):
        sent = send[k].at[pl.ds(0, total - fr_dev)]
        pltpu.make_async_copy(sent, sent, send_sem.at[k]).wait()
        pltpu.make_async_copy(own[k], oth[k], swap_send.at[k]).wait()


def body(frames, cycle_map):
    fr_dev, p_sec = frames.shape
    cycles = lax.axis_size("frame")
    total = fr_dev * cycles
    blocks = p_sec // BLOCK
    rows = total // lax.axis_size("pix")
    cap = p_sec // cycles
    slots = cap // BLOCK
    chunks = chunks_of(slots)
    widths = [size * BLOCK for first, size in chunks]
    tile = min(256, total)
    dma = pltpu.SemaphoreType.DMA
    out = pl.pallas_call(
        functools.partial(kernel, cycles),
        out_shape=pltpu.VMEM((rows, total), jnp.bfloat16),
        in_specs=[pl.BlockSpec(memory_space=pltpu.HBM)] * 2,
        out_specs=pl.BlockSpec(memory_space=pltpu.VMEM),
        scratch_shapes=[
            pltpu.VMEM((fr_dev, p_sec + BLOCK), jnp.bfloat16),
            pltpu.VMEM((blocks + 8, BLOCK), jnp.int32),
            pltpu.VMEM((slots, BLOCK), jnp.int32),
            pltpu.SMEM((slots, BLOCK), jnp.int32),
            *[pltpu.VMEM((total, width), jnp.bfloat16) for width in widths],
            *[pltpu.VMEM((total + 2 * PAD, width), jnp.bfloat16) for width in widths],
            *[pltpu.VMEM((total, width), jnp.bfloat16) for width in widths],
            *[pltpu.VMEM((total, width), jnp.bfloat16) for width in widths],
            pltpu.VMEM((rows + PAD, total), jnp.float32),
            pltpu.VMEM((rows, BLOCK), jnp.float32),
            pltpu.VMEM((total, BLOCK), jnp.float32),
            pltpu.VMEM((tile, tile + 2 * PAD), jnp.bfloat16),
            pltpu.VMEM((8, cap), jnp.float32),
            pltpu.VMEM((8, BLOCK), jnp.float32),
            pltpu.VMEM((8, BLOCK), jnp.float32),
            dma((3,)),
            dma((len(chunks),)),
            dma((len(chunks),)),
            dma((len(chunks),)),
            dma((len(chunks),)),
            dma((2,)),
        ],
        compiler_params=pltpu.CompilerParams(
            collective_id=0, has_side_effects=True, vmem_limit_bytes=60 << 20
        ),
    )(frames, cycle_map.reshape(blocks, BLOCK))
    return out[None]


def solution(mesh):
    return jax.shard_map(
        body,
        mesh=mesh,
        in_specs=(P("frame", "pix"), P("pix")),
        out_specs=P("frame", "pix", None),
        check_vma=False,
    )
```

```python
import functools

import jax
import jax.numpy as jnp
from jax import lax
from jax.experimental import pallas as pl
from jax.experimental.pallas import tpu as pltpu
from jax.sharding import PartitionSpec as P

BLOCK = 128
HALF_WIN = 2
PAD = 16
SPLIT = (2, 2, 2, 2)
STRIDE = 11
MESH = pl.DeviceIdType.MESH


def chunks_of(slots):
    sizes = [size * slots // sum(SPLIT) for size in SPLIT]
    return [(sum(sizes[:k]), size) for k, size in enumerate(sizes)]


def kernel(
    cycles,
    frames_hbm,
    map_hbm,
    out_ref,
    fr,
    cmap,
    table_v,
    table,
    *refs,
):
    f = lax.axis_index("frame")
    p = lax.axis_index("pix")
    fr_dev = frames_hbm.shape[0]
    p_sec = frames_hbm.shape[1]
    blocks = p_sec // BLOCK
    total = fr_dev * cycles
    rows = total // 2
    slots = p_sec // cycles // BLOCK
    chunks = chunks_of(slots)
    count = len(chunks)
    tile = min(256, total)
    send, recv, own, oth = (refs[i * count : (i + 1) * count] for i in range(4))
    (
        acc,
        rowacc,
        inv_len,
        band,
        mask,
        cnt_own,
        cnt_oth,
        load_sem,
        send_sem,
        recv_sem,
        swap_send,
        swap_recv,
        cnt_sem,
    ) = refs[4 * count :]

    map_copy = pltpu.make_async_copy(map_hbm, cmap.at[pl.ds(0, blocks)], load_sem.at[0])
    map_copy.start()
    fr_copy = pltpu.make_async_copy(frames_hbm, fr.at[:, pl.ds(0, p_sec)], load_sem.at[1])
    fr_copy.start()

    barrier = pltpu.get_barrier_semaphore()

    def greet(i, carry):
        peer = lax.rem(f + STRIDE * i, cycles)
        pl.semaphore_signal(barrier, inc=1, device_id=(peer, p), device_id_type=MESH)
        return carry

    steps = 7 if cycles % 7 == 1 else 1
    lax.fori_loop(1, cycles, greet, 0, unroll=steps)
    pl.semaphore_signal(barrier, inc=1, device_id=(f, 1 - p), device_id_type=MESH)

    fr[:, pl.ds(p_sec, BLOCK)] = jnp.zeros((fr_dev, BLOCK), jnp.bfloat16)
    cmap[pl.ds(blocks, 8), :] = jnp.full((8, BLOCK), -1, jnp.int32)
    map_copy.wait()
    lane = lax.broadcasted_iota(jnp.int32, (8, BLOCK), 1)
    lead = lax.broadcasted_iota(jnp.int32, (8, BLOCK), 0)
    running = jnp.zeros((8, BLOCK), jnp.int32)
    member = []
    before = []
    for v in range(blocks // 8):
        member.append(jnp.broadcast_to(cmap[pl.ds(8 * v, 8), 0:1], (8, BLOCK)) == lane)
        before.append(running)
        running = running + jnp.where(member[v], 1, 0)
    ahead = [jnp.zeros((1, BLOCK), jnp.int32)]
    for i in range(7):
        ahead.append(ahead[i] + running[i : i + 1, :])
    ahead = jnp.concatenate(ahead, axis=0)
    picks = [jnp.zeros((8, BLOCK), jnp.int32)] * slots
    for v in range(blocks // 8):
        rank = jnp.where(member[v], before[v] + ahead, -1)
        for r in range(slots):
            picks[r] = picks[r] + jnp.where(rank == r, lead + (8 * v + 1), 0)
    found = jnp.concatenate([jnp.sum(x, axis=0, keepdims=True) for x in picks], axis=0)
    table_v[...] = jnp.where(found > 0, found - 1, blocks)
    table_copy = pltpu.make_async_copy(table_v, table, load_sem.at[2])
    table_copy.start()
    table_copy.wait()
    fr_copy.wait()

    def pick(k):
        def one(q, carry):
            for j in range(chunks[k][1]):
                b = table[chunks[k][0] + j, q]
                send[k][pl.ds(pl.multiple_of(q * fr_dev, fr_dev), fr_dev), pl.ds(j * BLOCK, BLOCK)] = fr[
                    :, pl.ds(b * BLOCK, BLOCK)
                ]
            return carry

        lax.fori_loop(0, cycles, one, 0, unroll=8 if cycles % 8 == 0 else 1)

    def ship(k):
        def one(i, carry):
            peer = lax.rem(f + STRIDE * i, cycles)
            pltpu.make_async_remote_copy(
                src_ref=send[k].at[pl.ds(pl.multiple_of(peer * fr_dev, fr_dev), fr_dev)],
                dst_ref=recv[k].at[pl.ds(pl.multiple_of(PAD + f * fr_dev, fr_dev), fr_dev)],
                send_sem=send_sem.at[k],
                recv_sem=recv_sem.at[k],
                device_id=(peer, p),
                device_id_type=MESH,
            ).start()
            return carry

        lax.fori_loop(1, cycles, one, 0, unroll=steps)
        recv[k][pl.ds(pl.multiple_of(PAD + f * fr_dev, fr_dev), fr_dev), :] = send[k][
            pl.ds(pl.multiple_of(f * fr_dev, fr_dev), fr_dev), :
        ]

    pick(0)
    pl.semaphore_wait(barrier, cycles)
    ship(0)
    for k in range(1, count):
        pick(k)
        ship(k)

    number = jnp.zeros((1, BLOCK), jnp.float32)
    for r in range(slots):
        row = (cmap[pl.ds(table[r, f], 1), :] == f).astype(jnp.float32)
        number = number + row
        mask[:, pl.ds(r * BLOCK, BLOCK)] = jnp.broadcast_to(row, (8, BLOCK))
    cnt_own[...] = jnp.broadcast_to(jnp.sum(number, axis=1, keepdims=True), (8, BLOCK))
    cnt_copy = pltpu.make_async_remote_copy(
        src_ref=cnt_own,
        dst_ref=cnt_oth,
        send_sem=cnt_sem.at[0],
        recv_sem=cnt_sem.at[1],
        device_id=(f, 1 - p),
        device_id_type=MESH,
    )
    cnt_copy.start()

    for k in range(count):
        zero_pad = jnp.zeros((PAD, chunks[k][1] * BLOCK), jnp.bfloat16)
        recv[k][pl.ds(0, PAD), :] = zero_pad
        recv[k][pl.ds(PAD + total, PAD), :] = zero_pad
    pos = lax.broadcasted_iota(jnp.int32, (total, BLOCK), 0)
    frames_in = jnp.minimum(pos + HALF_WIN, total - 1) - jnp.maximum(pos - HALF_WIN, 0) + 1
    inv_len[...] = 1.0 / frames_in.astype(jnp.float32)
    away = lax.broadcasted_iota(jnp.int32, (tile, tile + 2 * PAD), 1) - PAD - lax.broadcasted_iota(
        jnp.int32, (tile, tile + 2 * PAD), 0
    )
    band[...] = (jnp.abs(away) <= HALF_WIN).astype(jnp.float32).astype(jnp.bfloat16)
    first_row = pl.multiple_of(p * rows, rows)

    def normalise(k):
        valid = mask[0:1, pl.ds(chunks[k][0] * BLOCK, chunks[k][1] * BLOCK)] > 0.0

        for j in range(total // tile):
            start = j * tile
            summed = jnp.dot(
                band[...], recv[k][pl.ds(start, tile + 2 * PAD), :], preferred_element_type=jnp.float32
            )
            scale = inv_len[pl.ds(start, tile), :]
            mean = summed * jnp.concatenate([scale] * chunks[k][1], axis=1)
            value = recv[k][pl.ds(start + PAD, tile), :].astype(jnp.float32)
            normed = jnp.where(valid, value / mean, 0.0)
            own[k][pl.ds(start, tile), :] = normed.astype(jnp.bfloat16)
            pltpu.make_async_remote_copy(
                src_ref=own[k].at[pl.ds(start, tile)],
                dst_ref=oth[k].at[pl.ds(start, tile)],
                send_sem=swap_send.at[k],
                recv_sem=swap_recv.at[k],
                device_id=(f, 1 - p),
                device_id_type=MESH,
            ).start()

    def side_by_side(parts, start, length):
        return jnp.concatenate([ref[pl.ds(start, length), :] for ref in parts], axis=1)

    def products(parts, n):
        left = side_by_side(parts, first_row, rows)
        ones_rows = jnp.ones((PAD, left.shape[1]), jnp.bfloat16)
        return lax.dot_general(
            jnp.concatenate([left, ones_rows], axis=0),
            side_by_side(parts, n * tile, tile),
            (((1,), (1,)), ((), ())),
            preferred_element_type=jnp.float32,
        )

    def row_sums(parts):
        left = side_by_side(parts, first_row, rows)
        ones_cols = jnp.ones((left.shape[1], BLOCK), jnp.bfloat16)
        return jnp.dot(left, ones_cols, preferred_element_type=jnp.float32)

    def gram(parts, first):
        rowacc[...] = row_sums(parts) if first else rowacc[...] + row_sums(parts)
        for n in range(total // tile):
            columns = pl.ds(n * tile, tile)
            term = products(parts, n)
            acc[:, columns] = term if first else acc[:, columns] + term

    def swapped(k):
        pltpu.make_async_copy(own[k], oth[k], swap_recv.at[k]).wait()

    for k in range(count):
        arrived = recv[k].at[pl.ds(0, total - fr_dev)]
        pltpu.make_async_copy(arrived, arrived, recv_sem.at[k]).wait()
        normalise(k)
        if k > 0:
            swapped(k - 1)
        gram([own[k]] if k == 0 else [oth[k - 1], own[k]], k == 0)

    last = count - 1
    cnt_copy.wait()
    members = cnt_own[0:1, 0:1] + cnt_oth[0:1, 0:1]
    swapped(last)
    row_total = rowacc[...] + row_sums([oth[last]])
    if tile > BLOCK:
        row_total = jnp.concatenate([row_total] * (tile // BLOCK), axis=1)
    else:
        row_total = row_total[:, :tile]
    for n in range(total // tile):
        columns = pl.ds(n * tile, tile)
        sums = acc[:, columns] + products([oth[last]], n)
        result = members * sums[:rows] / (row_total * sums[rows : rows + 1, :]) - 1.0
        out_ref[:, columns] = result.astype(jnp.bfloat16)

    for k in range(count):
        sent = send[k].at[pl.ds(0, total - fr_dev)]
        pltpu.make_async_copy(sent, sent, send_sem.at[k]).wait()
        pltpu.make_async_copy(own[k], oth[k], swap_send.at[k]).wait()


def body(frames, cycle_map):
    fr_dev, p_sec = frames.shape
    cycles = lax.axis_size("frame")
    total = fr_dev * cycles
    blocks = p_sec // BLOCK
    rows = total // lax.axis_size("pix")
    cap = p_sec // cycles
    slots = cap // BLOCK
    chunks = chunks_of(slots)
    widths = [size * BLOCK for first, size in chunks]
    tile = min(256, total)
    dma = pltpu.SemaphoreType.DMA
    out = pl.pallas_call(
        functools.partial(kernel, cycles),
        out_shape=pltpu.VMEM((rows, total), jnp.bfloat16),
        in_specs=[pl.BlockSpec(memory_space=pltpu.HBM)] * 2,
        out_specs=pl.BlockSpec(memory_space=pltpu.VMEM),
        scratch_shapes=[
            pltpu.VMEM((fr_dev, p_sec + BLOCK), jnp.bfloat16),
            pltpu.VMEM((blocks + 8, BLOCK), jnp.int32),
            pltpu.VMEM((slots, BLOCK), jnp.int32),
            pltpu.SMEM((slots, BLOCK), jnp.int32),
            *[pltpu.VMEM((total, width), jnp.bfloat16) for width in widths],
            *[pltpu.VMEM((total + 2 * PAD, width), jnp.bfloat16) for width in widths],
            *[pltpu.VMEM((total, width), jnp.bfloat16) for width in widths],
            *[pltpu.VMEM((total, width), jnp.bfloat16) for width in widths],
            pltpu.VMEM((rows + PAD, total), jnp.float32),
            pltpu.VMEM((rows, BLOCK), jnp.float32),
            pltpu.VMEM((total, BLOCK), jnp.float32),
            pltpu.VMEM((tile, tile + 2 * PAD), jnp.bfloat16),
            pltpu.VMEM((8, cap), jnp.float32),
            pltpu.VMEM((8, BLOCK), jnp.float32),
            pltpu.VMEM((8, BLOCK), jnp.float32),
            dma((3,)),
            dma((len(chunks),)),
            dma((len(chunks),)),
            dma((len(chunks),)),
            dma((len(chunks),)),
            dma((2,)),
        ],
        compiler_params=pltpu.CompilerParams(
            collective_id=0, has_side_effects=True, vmem_limit_bytes=60 << 20
        ),
    )(frames, cycle_map.reshape(blocks, BLOCK))
    return out[None]


def solution(mesh):
    return jax.shard_map(
        body,
        mesh=mesh,
        in_specs=(P("frame", "pix"), P("pix")),
        out_specs=P("frame", "pix", None),
        check_vma=False,
    )
```

```python
import functools

import jax
import jax.numpy as jnp
from jax import lax
from jax.experimental import pallas as pl
from jax.experimental.pallas import tpu as pltpu
from jax.sharding import PartitionSpec as P

BLOCK = 128
HALF_WIN = 2
PAD = 16
SPLIT = (3, 3, 2)
STRIDE = 11
MESH = pl.DeviceIdType.MESH


def chunks_of(slots):
    sizes = [size * slots // sum(SPLIT) for size in SPLIT]
    return [(sum(sizes[:k]), size) for k, size in enumerate(sizes)]


def kernel(
    cycles,
    frames_hbm,
    map_hbm,
    out_ref,
    fr,
    cmap,
    table_v,
    table,
    *refs,
):
    f = lax.axis_index("frame")
    p = lax.axis_index("pix")
    fr_dev = frames_hbm.shape[0]
    p_sec = frames_hbm.shape[1]
    blocks = p_sec // BLOCK
    total = fr_dev * cycles
    rows = total // 2
    slots = p_sec // cycles // BLOCK
    chunks = chunks_of(slots)
    count = len(chunks)
    tile = min(256, total)
    send, recv, own, oth = (refs[i * count : (i + 1) * count] for i in range(4))
    (
        acc,
        rowacc,
        inv_len,
        band,
        mask,
        cnt_own,
        cnt_oth,
        load_sem,
        send_sem,
        recv_sem,
        swap_send,
        swap_recv,
        cnt_sem,
    ) = refs[4 * count :]

    map_copy = pltpu.make_async_copy(map_hbm, cmap.at[pl.ds(0, blocks)], load_sem.at[0])
    map_copy.start()
    fr_copy = pltpu.make_async_copy(frames_hbm, fr.at[:, pl.ds(0, p_sec)], load_sem.at[1])
    fr_copy.start()

    barrier = pltpu.get_barrier_semaphore()

    def greet(i, carry):
        peer = lax.rem(f + STRIDE * i, cycles)
        pl.semaphore_signal(barrier, inc=1, device_id=(peer, p), device_id_type=MESH)
        return carry

    steps = 7 if cycles % 7 == 1 else 1
    lax.fori_loop(1, cycles, greet, 0, unroll=steps)
    pl.semaphore_signal(barrier, inc=1, device_id=(f, 1 - p), device_id_type=MESH)

    fr[:, pl.ds(p_sec, BLOCK)] = jnp.zeros((fr_dev, BLOCK), jnp.bfloat16)
    cmap[pl.ds(blocks, 8), :] = jnp.full((8, BLOCK), -1, jnp.int32)
    map_copy.wait()
    lane = lax.broadcasted_iota(jnp.int32, (8, BLOCK), 1)
    lead = lax.broadcasted_iota(jnp.int32, (8, BLOCK), 0)
    running = jnp.zeros((8, BLOCK), jnp.int32)
    member = []
    before = []
    for v in range(blocks // 8):
        member.append(jnp.broadcast_to(cmap[pl.ds(8 * v, 8), 0:1], (8, BLOCK)) == lane)
        before.append(running)
        running = running + jnp.where(member[v], 1, 0)
    ahead = [jnp.zeros((1, BLOCK), jnp.int32)]
    for i in range(7):
        ahead.append(ahead[i] + running[i : i + 1, :])
    ahead = jnp.concatenate(ahead, axis=0)
    picks = [jnp.zeros((8, BLOCK), jnp.int32)] * slots
    for v in range(blocks // 8):
        rank = jnp.where(member[v], before[v] + ahead, -1)
        for r in range(slots):
            picks[r] = picks[r] + jnp.where(rank == r, lead + (8 * v + 1), 0)
    found = jnp.concatenate([jnp.sum(x, axis=0, keepdims=True) for x in picks], axis=0)
    table_v[...] = jnp.where(found > 0, found - 1, blocks)
    table_copy = pltpu.make_async_copy(table_v, table, load_sem.at[2])
    table_copy.start()
    table_copy.wait()
    fr_copy.wait()

    def pick(k):
        def one(q, carry):
            for j in range(chunks[k][1]):
                b = table[chunks[k][0] + j, q]
                send[k][pl.ds(pl.multiple_of(q * fr_dev, fr_dev), fr_dev), pl.ds(j * BLOCK, BLOCK)] = fr[
                    :, pl.ds(b * BLOCK, BLOCK)
                ]
            return carry

        lax.fori_loop(0, cycles, one, 0, unroll=8 if cycles % 8 == 0 else 1)

    def ship(k):
        def one(i, carry):
            peer = lax.rem(f + STRIDE * i, cycles)
            pltpu.make_async_remote_copy(
                src_ref=send[k].at[pl.ds(pl.multiple_of(peer * fr_dev, fr_dev), fr_dev)],
                dst_ref=recv[k].at[pl.ds(pl.multiple_of(PAD + f * fr_dev, fr_dev), fr_dev)],
                send_sem=send_sem.at[k],
                recv_sem=recv_sem.at[k],
                device_id=(peer, p),
                device_id_type=MESH,
            ).start()
            return carry

        lax.fori_loop(1, cycles, one, 0, unroll=steps)
        recv[k][pl.ds(pl.multiple_of(PAD + f * fr_dev, fr_dev), fr_dev), :] = send[k][
            pl.ds(pl.multiple_of(f * fr_dev, fr_dev), fr_dev), :
        ]

    pick(0)
    pl.semaphore_wait(barrier, cycles)
    ship(0)
    for k in range(1, count):
        pick(k)
        ship(k)

    number = jnp.zeros((1, BLOCK), jnp.float32)
    for r in range(slots):
        row = (cmap[pl.ds(table[r, f], 1), :] == f).astype(jnp.float32)
        number = number + row
        mask[:, pl.ds(r * BLOCK, BLOCK)] = jnp.broadcast_to(row, (8, BLOCK))
    cnt_own[...] = jnp.broadcast_to(jnp.sum(number, axis=1, keepdims=True), (8, BLOCK))
    cnt_copy = pltpu.make_async_remote_copy(
        src_ref=cnt_own,
        dst_ref=cnt_oth,
        send_sem=cnt_sem.at[0],
        recv_sem=cnt_sem.at[1],
        device_id=(f, 1 - p),
        device_id_type=MESH,
    )
    cnt_copy.start()

    for k in range(count):
        zero_pad = jnp.zeros((PAD, chunks[k][1] * BLOCK), jnp.bfloat16)
        recv[k][pl.ds(0, PAD), :] = zero_pad
        recv[k][pl.ds(PAD + total, PAD), :] = zero_pad
    pos = lax.broadcasted_iota(jnp.int32, (total, BLOCK), 0)
    frames_in = jnp.minimum(pos + HALF_WIN, total - 1) - jnp.maximum(pos - HALF_WIN, 0) + 1
    inv_len[...] = 1.0 / frames_in.astype(jnp.float32)
    away = lax.broadcasted_iota(jnp.int32, (tile, tile + 2 * PAD), 1) - PAD - lax.broadcasted_iota(
        jnp.int32, (tile, tile + 2 * PAD), 0
    )
    band[...] = (jnp.abs(away) <= HALF_WIN).astype(jnp.float32).astype(jnp.bfloat16)
    first_row = pl.multiple_of(p * rows, rows)

    def normalise(k):
        valid = mask[0:1, pl.ds(chunks[k][0] * BLOCK, chunks[k][1] * BLOCK)] > 0.0

        for j in range(total // tile):
            start = j * tile
            summed = jnp.dot(
                band[...], recv[k][pl.ds(start, tile + 2 * PAD), :], preferred_element_type=jnp.float32
            )
            scale = inv_len[pl.ds(start, tile), :]
            mean = summed * jnp.concatenate([scale] * chunks[k][1], axis=1)
            value = recv[k][pl.ds(start + PAD, tile), :].astype(jnp.float32)
            normed = jnp.where(valid, value / mean, 0.0)
            own[k][pl.ds(start, tile), :] = normed.astype(jnp.bfloat16)
            pltpu.make_async_remote_copy(
                src_ref=own[k].at[pl.ds(start, tile)],
                dst_ref=oth[k].at[pl.ds(start, tile)],
                send_sem=swap_send.at[k],
                recv_sem=swap_recv.at[k],
                device_id=(f, 1 - p),
                device_id_type=MESH,
            ).start()

    def side_by_side(parts, start, length):
        return jnp.concatenate([ref[pl.ds(start, length), :] for ref in parts], axis=1)

    def products(parts, n):
        left = side_by_side(parts, first_row, rows)
        ones_rows = jnp.ones((PAD, left.shape[1]), jnp.bfloat16)
        return lax.dot_general(
            jnp.concatenate([left, ones_rows], axis=0),
            side_by_side(parts, n * tile, tile),
            (((1,), (1,)), ((), ())),
            preferred_element_type=jnp.float32,
        )

    def row_sums(parts):
        left = side_by_side(parts, first_row, rows)
        ones_cols = jnp.ones((left.shape[1], BLOCK), jnp.bfloat16)
        return jnp.dot(left, ones_cols, preferred_element_type=jnp.float32)

    def gram(parts, first):
        rowacc[...] = row_sums(parts) if first else rowacc[...] + row_sums(parts)
        for n in range(total // tile):
            columns = pl.ds(n * tile, tile)
            term = products(parts, n)
            acc[:, columns] = term if first else acc[:, columns] + term

    def swapped(k):
        pltpu.make_async_copy(own[k], oth[k], swap_recv.at[k]).wait()

    for k in range(count):
        arrived = recv[k].at[pl.ds(0, total - fr_dev)]
        pltpu.make_async_copy(arrived, arrived, recv_sem.at[k]).wait()
        normalise(k)
        if k > 0:
            swapped(k - 1)
        gram([own[k]] if k == 0 else [oth[k - 1], own[k]], k == 0)

    last = count - 1
    cnt_copy.wait()
    members = cnt_own[0:1, 0:1] + cnt_oth[0:1, 0:1]
    swapped(last)
    row_total = rowacc[...] + row_sums([oth[last]])
    if tile > BLOCK:
        row_total = jnp.concatenate([row_total] * (tile // BLOCK), axis=1)
    else:
        row_total = row_total[:, :tile]
    for n in range(total // tile):
        columns = pl.ds(n * tile, tile)
        sums = acc[:, columns] + products([oth[last]], n)
        result = members * sums[:rows] / (row_total * sums[rows : rows + 1, :]) - 1.0
        out_ref[:, columns] = result.astype(jnp.bfloat16)

    for k in range(count):
        sent = send[k].at[pl.ds(0, total - fr_dev)]
        pltpu.make_async_copy(sent, sent, send_sem.at[k]).wait()
        pltpu.make_async_copy(own[k], oth[k], swap_send.at[k]).wait()


def body(frames, cycle_map):
    fr_dev, p_sec = frames.shape
    cycles = lax.axis_size("frame")
    total = fr_dev * cycles
    blocks = p_sec // BLOCK
    rows = total // lax.axis_size("pix")
    cap = p_sec // cycles
    slots = cap // BLOCK
    chunks = chunks_of(slots)
    widths = [size * BLOCK for first, size in chunks]
    tile = min(256, total)
    dma = pltpu.SemaphoreType.DMA
    out = pl.pallas_call(
        functools.partial(kernel, cycles),
        out_shape=pltpu.VMEM((rows, total), jnp.bfloat16),
        in_specs=[pl.BlockSpec(memory_space=pltpu.HBM)] * 2,
        out_specs=pl.BlockSpec(memory_space=pltpu.VMEM),
        scratch_shapes=[
            pltpu.VMEM((fr_dev, p_sec + BLOCK), jnp.bfloat16),
            pltpu.VMEM((blocks + 8, BLOCK), jnp.int32),
            pltpu.VMEM((slots, BLOCK), jnp.int32),
            pltpu.SMEM((slots, BLOCK), jnp.int32),
            *[pltpu.VMEM((total, width), jnp.bfloat16) for width in widths],
            *[pltpu.VMEM((total + 2 * PAD, width), jnp.bfloat16) for width in widths],
            *[pltpu.VMEM((total, width), jnp.bfloat16) for width in widths],
            *[pltpu.VMEM((total, width), jnp.bfloat16) for width in widths],
            pltpu.VMEM((rows + PAD, total), jnp.float32),
            pltpu.VMEM((rows, BLOCK), jnp.float32),
            pltpu.VMEM((total, BLOCK), jnp.float32),
            pltpu.VMEM((tile, tile + 2 * PAD), jnp.bfloat16),
            pltpu.VMEM((8, cap), jnp.float32),
            pltpu.VMEM((8, BLOCK), jnp.float32),
            pltpu.VMEM((8, BLOCK), jnp.float32),
            dma((3,)),
            dma((len(chunks),)),
            dma((len(chunks),)),
            dma((len(chunks),)),
            dma((len(chunks),)),
            dma((2,)),
        ],
        compiler_params=pltpu.CompilerParams(
            collective_id=0, has_side_effects=True, vmem_limit_bytes=60 << 20
        ),
    )(frames, cycle_map.reshape(blocks, BLOCK))
    return out[None]


def solution(mesh):
    return jax.shard_map(
        body,
        mesh=mesh,
        in_specs=(P("frame", "pix"), P("pix")),
        out_specs=P("frame", "pix", None),
        check_vma=False,
    )
```
